256 devices in a mesh: tok: 64 (over z, x, core), grp: 4 (over y).
Axes of the slice: x: 4, y: 4, z: 8, core: 2. Of those that a mesh axis runs over, the one named last changes fastest.
Arguments:
- queries: bfloat16 [4, 8192, 3072], P('grp', 'tok'), may hold values from -20 to 20, as said below
- keys: bfloat16 [4, 8192, 3072], P('grp', 'tok'), may hold values from -20 to 20, as said below
- values: bfloat16 [4, 8192, 3072], P('grp', 'tok'), may hold values from -10 to 10, as said below
- next_latent: bfloat16 [4, 8192, 3072], P('grp', 'tok'), may hold values from -20 to 20, as said below
- clip_blocks: int32 [4, 16], P('grp'), may hold values from 1 to 8, 64 in all within a row
- valid_counts: int32 [4, 64], P('grp'), may hold values from 32 to 128
- group_ids: int32 [4, 16], P('grp'), may hold values from 0 to 3
- rewards: float32 [4, 16], P('grp'), may hold values from -6 to 6
Outputs:
- velocity: bfloat16 [4, 8192, 3072], P('grp', 'tok')
- loss: float32 [], replicated
The draws below stay inside these ranges and needn't reach their ends.
Inputs may be any that keep to these rules, and one draw needn't show every extreme that they name: queries drawn within the range. keys drawn within the range. values drawn within the range. `next_latent`: next latents drawn within the range.
All inputs are finite; a program needn't handle non-finite values.
Results may differ from the reference program's by a relative error of at most 0.0034.
Values may be sent and summed in bfloat16 or wider, within the bound.
A program may use at most 128 MiB of HBM per device.

```python
import math
import jax
import jax.numpy as jnp
import numpy as np
from jax import lax

D = 3072
HEADS = 24
HEAD = 128
BLK = 128
MAXB = 8
GROUPS = 4
NBT = 64
TOKENS = 8192
CLIPS = 16
N_GRP = 4


def paired_draw(key):
    shape = (N_GRP, TOKENS, D)
    key_part = jax.random.truncated_normal(jax.random.fold_in(key, 11), -6.0, 6.0, shape, jnp.float32)
    query_part = jax.random.truncated_normal(jax.random.fold_in(key, 12), -6.0, 6.0, shape, jnp.float32)
    return (query_part, key_part)


def draw_queries(key, part):
    return paired_draw(key)[0].astype(jnp.bfloat16)


def draw_keys(key, part):
    return paired_draw(key)[1].astype(jnp.bfloat16)


def draw_values(key, part):
    means_shape = (N_GRP, NBT, 1, D)
    noise_shape = (N_GRP, NBT, BLK, D)
    means = jax.random.truncated_normal(jax.random.fold_in(key, 32), -4.0, 4.0, means_shape, jnp.float32)
    noise = jax.random.truncated_normal(jax.random.fold_in(key, 33), -6.0, 6.0, noise_shape, jnp.float32)
    return (means + noise).reshape(N_GRP, TOKENS, D).astype(jnp.bfloat16)


def draw_next_latent(key, part):
    block_shape = (N_GRP, NBT, 1, 1)
    logs = jax.random.uniform(jax.random.fold_in(key, 21), block_shape, jnp.float32, jnp.log(0.3), jnp.log(3.0))
    noise = jax.random.truncated_normal(jax.random.fold_in(key, 22), -6.0, 6.0, (N_GRP, NBT, BLK, D), jnp.float32)
    latent = jnp.exp(logs) * noise
    return latent.reshape(N_GRP, TOKENS, D).astype(jnp.bfloat16)


def plant(result, stream_key, smallest, high):
    longest = result.shape.index(max(result.shape))
    spots = []
    for shift in (0, 1):
        where = [jax.random.randint(jax.random.fold_in(stream_key, axis), (), 0, length) for axis, length in enumerate(result.shape)]
        where[longest] = (where[longest] + shift) % result.shape[longest]
        spots.append(tuple(where))
    return result.at[spots[0]].set(smallest).at[spots[1]].set(high)


def block_levels(stream_key, shape, cuts, least, top_value):
    level, own = 1.0, jax.random.fold_in(stream_key, 6)
    for position, parts in cuts:
        steps = jnp.exp(jax.random.uniform(jax.random.fold_in(own, position), (parts,), jnp.float32, least / len(cuts), top_value / len(cuts)))
        level = level * jnp.repeat(steps, shape[position] // parts).reshape([-1 if axis == position else 1 for axis in range(len(shape))])
    return level


def profile(amount, total, most, slope):
    loads = [(1 << 20) // math.isqrt(standing ** slope) + 1 for standing in range(2, amount + 1)]
    spare, given = total - most - (amount - 1), [1] * (amount - 1)
    while spare > 0:
        candidates = [i for i in range(amount - 1) if given[i] < most]
        mass, budget = sum([loads[i] for i in candidates]), spare
        for i in candidates:
            more = min(most - given[i], max(1, budget * loads[i] // mass), spare)
            given[i] = given[i] + more
            spare = spare - more
    return np.array([most] + given)


def ragged(rng, count, total, limit, slope):
    if count == 2:
        one = jax.random.randint(rng, (), max(1, total - limit), min(limit, total - 1) + 1)
        return jnp.stack([one, total - one])
    tallies = jnp.asarray(profile(count, total, limit, slope), jnp.int32)
    twos = (count - 1) // 2
    giver, taker = tallies[1:1 + 2 * twos:2], tallies[2:2 + 2 * twos:2]
    slack = jnp.minimum(giver - 1, limit - taker)
    moved = jax.random.randint(jax.random.fold_in(rng, 1), (twos,), 0, 1 << 20) % (slack + 1)
    tallies = tallies.at[1:1 + 2 * twos:2].set(giver - moved).at[2:2 + 2 * twos:2].set(taker + moved)
    return tallies[jax.random.permutation(jax.random.fold_in(rng, 2), count)]


def gaussian(stream_key, shape, deviation, reach, pieces=(), held_as=jnp.bfloat16):
    array = jax.random.normal(stream_key, shape, jnp.float32) * deviation
    if len(pieces) > 0:
        array = block_levels(stream_key, shape, pieces, -0.22, 0.18) * array
    return jnp.clip(array, min=-reach, max=reach).astype(held_as)


def setup_inputs(seed: int = 0) -> dict:
    arg_keys = jax.random.split(jax.random.key(seed), 9)
    return {
        "queries": draw_queries(jax.random.fold_in(arg_keys[8], 71), 0),
        "keys": draw_keys(jax.random.fold_in(arg_keys[8], 71), 0),
        "values": draw_values(jax.random.fold_in(arg_keys[8], 71), 0),
        "next_latent": draw_next_latent(jax.random.fold_in(arg_keys[8], 71), 0),
        "clip_blocks": jax.vmap(lambda own: ragged(own, CLIPS, NBT, MAXB, 1))(jax.random.split(arg_keys[4], N_GRP)).reshape((N_GRP, CLIPS)).astype(jnp.int32),
        "valid_counts": plant(jax.random.randint(arg_keys[5], (N_GRP, NBT), BLK // 4, BLK + 1), jax.random.fold_in(arg_keys[5], 1), BLK // 4, BLK).astype(jnp.int32),
        "group_ids": plant(jax.random.randint(arg_keys[6], (N_GRP, CLIPS), 0, GROUPS), jax.random.fold_in(arg_keys[6], 1), 0, GROUPS - 1).astype(jnp.int32),
        "rewards": gaussian(arg_keys[7], (N_GRP, CLIPS), 1.0, 6.0, ((0, 4),), jnp.float32),
    }


masked_score = -1e+30

def block_clips(clip_row, total_blocks):
    ends = jnp.cumsum(clip_row).astype(jnp.int32)
    positions = jnp.arange(total_blocks, dtype=jnp.int32)
    return lax.optimization_barrier(jnp.sum((ends[None, :] <= positions[:, None]).astype(jnp.int32), axis=1)).astype(jnp.int32)

def advantages(reward_row, group_row):
    member = (group_row[:, None] == jnp.arange(GROUPS, dtype=jnp.int32)[None, :]).astype(jnp.float32)
    totals = lax.optimization_barrier(jnp.sum(member * reward_row[:, None], axis=0))
    counts = lax.optimization_barrier(jnp.sum(member, axis=0))
    means = totals / jnp.maximum(counts, 1.0)
    return reward_row - lax.optimization_barrier(jnp.sum(member * means[None, :], axis=1))

def clip_tokens(block_clip, valid_row, clips):
    member = (block_clip[:, None] == jnp.arange(clips, dtype=jnp.int32)[None, :]).astype(jnp.float32)
    return lax.optimization_barrier(jnp.sum(member * valid_row.astype(jnp.float32)[:, None], axis=0))

def attend(query_block, key_rows, value_rows, allowed):
    width = query_block.shape[0]
    count = key_rows.shape[0]
    query_heads = query_block.reshape(width, HEADS, HEAD).astype(jnp.float32)
    key_heads = key_rows.reshape(count, HEADS, HEAD).astype(jnp.float32)
    value_heads = value_rows.reshape(count, HEADS, HEAD).astype(jnp.float32)
    scores = jnp.einsum('qhd,khd->hqk', query_heads, key_heads) * (1.0 / math.sqrt(HEAD))
    scores = jnp.where(allowed[None, None, :], scores, masked_score)
    top = lax.optimization_barrier(jnp.max(scores, axis=-1, keepdims=True))
    expo = jnp.exp(scores - top)
    probs = (expo / lax.optimization_barrier(jnp.sum(expo, axis=-1, keepdims=True))).astype(jnp.bfloat16)
    mixed = jnp.einsum('hqk,khd->qhd', probs.astype(jnp.float32), value_heads)
    return mixed.reshape(width, HEADS * HEAD)

def row_velocity(query_row, key_row, value_row, clip_row, valid_row):
    total_blocks = valid_row.shape[0]
    block_clip = block_clips(clip_row, total_blocks)
    margin = (MAXB - 1) * BLK
    key_padded = jnp.pad(key_row, ((margin, margin), (0, 0)))
    value_padded = jnp.pad(value_row, ((margin, margin), (0, 0)))
    clip_padded = jnp.pad(block_clip, (MAXB - 1, MAXB - 1), constant_values=-1)
    valid_padded = jnp.pad(valid_row, (MAXB - 1, MAXB - 1))
    span = 2 * MAXB - 1

    def one_block(block):
        start = (block * BLK).astype(jnp.int32)
        query_block = lax.dynamic_slice_in_dim(query_row, start, BLK, 0)
        key_block = lax.dynamic_slice_in_dim(key_padded, start, span * BLK, 0)
        value_block = lax.dynamic_slice_in_dim(value_padded, start, span * BLK, 0)
        near_clips = lax.dynamic_slice_in_dim(clip_padded, block, span, 0)
        near_valid = lax.dynamic_slice_in_dim(valid_padded, block, span, 0)
        slots = jnp.arange(BLK, dtype=jnp.int32)
        allowed = (near_clips[:, None] == block_clip[block]) & (slots[None, :] < near_valid[:, None])
        mixed = attend(query_block, key_block, value_block, allowed.reshape(-1))
        live = slots < valid_row[block]
        return jnp.where(live[:, None], mixed, 0.0).astype(jnp.bfloat16)
    outputs = lax.map(one_block, jnp.arange(total_blocks, dtype=jnp.int32))
    return outputs.reshape(total_blocks * BLK, D)

def row_loss(velocity_row, next_row, clip_row, valid_row, group_row, reward_row):
    total_blocks = valid_row.shape[0]
    block_clip = block_clips(clip_row, total_blocks)
    diff = next_row.astype(jnp.float32) - velocity_row.astype(jnp.float32)
    token_err = lax.optimization_barrier(jnp.sum(diff * diff, axis=-1)).reshape(total_blocks, BLK)
    slots = jnp.arange(BLK, dtype=jnp.int32)
    live = (slots[None, :] < valid_row[:, None]).astype(jnp.float32)
    block_err = lax.optimization_barrier(jnp.sum(token_err * live, axis=1))
    adv = advantages(reward_row, group_row)
    tokens_of = clip_tokens(block_clip, valid_row, clip_row.shape[0])
    terms = jnp.take(adv, block_clip) * block_err / (2.0 * D * jnp.take(tokens_of, block_clip))
    return jnp.sum(terms)

def reference(queries, keys, values, next_latent, clip_blocks, valid_counts, group_ids, rewards):
    outputs = []
    total = jnp.zeros((), jnp.float32)
    for row in range(queries.shape[0]):
        velocity_row = row_velocity(queries[row], keys[row], values[row], clip_blocks[row], valid_counts[row])
        outputs.append(velocity_row)
        total = total + row_loss(velocity_row, next_latent[row], clip_blocks[row], valid_counts[row], group_ids[row], rewards[row])
    return (jnp.stack(outputs), total)
```

```python
import functools
import math

import jax
import jax.numpy as jnp
from jax import lax
from jax.experimental import pallas as pl
from jax.experimental.pallas import tpu as pltpu
from jax.sharding import Mesh
from jax.sharding import PartitionSpec as P

D = 3072
HEADS = 24
HEAD = 128
BLK = 128
MAXB = 8
ROW = 8
SHARE = HEADS // ROW
SPAN = MAXB * BLK
MASKED = -1e30
TILE = (8, 128)
MESH = pl.DeviceIdType.MESH


def rows_at(block):
    return pl.ds(pl.multiple_of(block * BLK, BLK), BLK)


def tables(sizes, clip_ref, valid_ref, group_ref, reward_ref, table_ref, weight_ref):
    nz, _ = sizes
    total_blocks = nz * ROW
    clips = clip_ref.shape[1]
    z, x, c = (lax.axis_index(a) for a in ("z", "x", "c"))
    own_block = z * ROW + x * 2 + c

    def clip_of(block):
        begin = start = count = own = jnp.int32(0)
        for i in range(clips):
            size = clip_ref[0, i]
            inside = (block >= begin) & (block < begin + size)
            start = jnp.where(inside, begin, start)
            count = jnp.where(inside, size, count)
            own = jnp.where(inside, i, own)
            begin = begin + size
        return start, count, own

    def note(i, carry):
        start, count, _ = clip_of(z * ROW + i)
        table_ref[0, i] = jnp.clip(start - (z * ROW - ROW), 0, 2 * ROW)
        table_ref[0, ROW + i] = valid_ref[0, z * ROW + i]
        for j in range(MAXB):
            live = valid_ref[0, jnp.minimum(start + j, total_blocks - 1)]
            table_ref[0, 2 * ROW + i * MAXB + j] = jnp.where(j < count, live, 0)
        return carry
    lax.fori_loop(0, ROW, note, 0)

    start, count, own = clip_of(own_block)
    group = group_ref[0, own]
    total, number = jnp.float32(0), jnp.float32(0)
    for i in range(clips):
        same = group_ref[0, i] == group
        total = total + jnp.where(same, reward_ref[0, i], 0.0)
        number = number + jnp.where(same, 1.0, 0.0)
    tokens = jnp.int32(0)
    for j in range(MAXB):
        live = valid_ref[0, jnp.minimum(start + j, total_blocks - 1)]
        tokens = tokens + jnp.where(j < count, live, 0)
    mean = jnp.full(TILE, total) / jnp.full(TILE, jnp.maximum(number, 1.0))
    adv = jnp.full(TILE, reward_ref[0, own]) - mean
    weight_ref[...] = adv / jnp.full(TILE, (2.0 * D) * tokens.astype(jnp.float32))


def kernel(sizes, q_hbm, k_hbm, v_hbm, next_hbm, table_ref, weight_ref,
           out_hbm, loss_ref, kb0, kb1, kb2, vb0, vb1, vb2, qb0, qb1, qb2, ob0, ob1, ob2,
           probs, got, nxt, red_x, red_y, red_z,
           xs, xr, us, ur, ds_, dr, os_, or_, misc, rs, rr):
    nz, ng = sizes
    z, x, c, g = (lax.axis_index(a) for a in ("z", "x", "c", "grp"))
    me = x * 2 + c
    keys, vals, qrys, outs = (kb0, kb1, kb2), (vb0, vb1, vb2), (qb0, qb1, qb2), (ob0, ob1, ob2)

    def row_dev(r):
        return {"x": r // 2, "c": lax.rem(r, 2)}

    def z_dev(dz):
        return {"z": lax.rem(z + dz, nz)}

    def g_dev(dg):
        return {"grp": lax.rem(g + dg, ng)}

    def source(kind):
        return (k_hbm, v_hbm, q_hbm)[kind // SHARE]

    def landing(kind, s):
        h = kind % SHARE
        if kind < 2 * SHARE:
            return (keys, vals)[kind // SHARE][h].at[ROW + s]
        return qrys[h].at[rows_at(s), :]

    def columns(r, h):
        return pl.ds(pl.multiple_of((r * SHARE + h) * HEAD, HEAD), HEAD)

    def share_copy(kind, d, s):
        r = lax.rem(me + d, ROW)
        return pltpu.make_async_remote_copy(
            src_ref=source(kind).at[0, :, columns(r, kind % SHARE)],
            dst_ref=landing(kind, s),
            send_sem=xs.at[kind, d], recv_sem=xr.at[kind, d],
            device_id=row_dev(r), device_id_type=MESH)

    def own_copy(kind):
        return pltpu.make_async_copy(
            source(kind).at[0, :, columns(me, kind % SHARE)], landing(kind, me), xr.at[kind, 0])

    def send_share(kind):
        own_copy(kind).start()

        def body(d, carry):
            share_copy(kind, d, me).start()
            return carry
        lax.fori_loop(1, ROW, body, 0)

    def sender(d):
        return lax.rem(me + ROW - d, ROW)

    def halo_copy(kind, s, d, up):
        buf = (keys, vals)[kind // SHARE][kind % SHARE]
        return pltpu.make_async_remote_copy(
            src_ref=buf.at[ROW + s],
            dst_ref=buf.at[s if up else 2 * ROW + s],
            send_sem=(us if up else ds_).at[kind, d], recv_sem=(ur if up else dr).at[kind, d],
            device_id=z_dev(1 if up else nz - 1), device_id_type=MESH)

    def for_halo(kind, s, d, act):
        @pl.when(s != 0)
        def _():
            act(halo_copy(kind, s, d, True))

        @pl.when(s != ROW - 1)
        def _():
            act(halo_copy(kind, s, d, False))

    def forward(kind):
        own_copy(kind).wait()
        for_halo(kind, me, 0, lambda copy: copy.start())

        def body(d, carry):
            s = sender(d)
            share_copy(kind, d, s).wait_recv()
            for_halo(kind, s, d, lambda copy: copy.start())
            return carry
        lax.fori_loop(1, ROW, body, 0)

    def wait_halo(kind):
        def body(d, carry):
            for_halo(kind, sender(d), d, lambda copy: copy.wait_recv())
            return carry
        lax.fori_loop(0, ROW, body, 0)

    def wait_queries(h):
        kind = 2 * SHARE + h
        own_copy(kind).wait()

        def body(d, carry):
            share_copy(kind, d, sender(d)).wait_recv()
            return carry
        lax.fori_loop(1, ROW, body, 0)

    barrier = pltpu.get_barrier_semaphore()
    partners = ([row_dev(lax.rem(me + d, ROW)) for d in range(1, ROW)]
                + [z_dev(d) for d in range(1, nz)] + [g_dev(d) for d in range(1, ng)])
    for device in partners:
        pl.semaphore_signal(barrier, inc=1, device_id=device, device_id_type=MESH)
    pl.semaphore_wait(barrier, len(partners))

    for kind in (0, 3, 1, 4, 6, 2, 5, 7, 8):
        send_share(kind)
    latent = pltpu.make_async_copy(next_hbm.at[0], nxt, misc.at[0])
    latent.start()

    lanes = lax.broadcasted_iota(jnp.int32, (1, BLK), 1)
    slots = lax.broadcasted_iota(jnp.int32, (BLK, HEAD), 0)

    def window(buf, i):
        first = table_ref[0, i]
        return jnp.concatenate([buf[first + j] for j in range(MAXB)], axis=0)

    def score(h):
        def body(i, carry):
            query = qrys[h][rows_at(i), :]
            key = window(keys[h], i)
            scores = lax.dot_general(query, key, (((1,), (1,)), ((), ())),
                                     preferred_element_type=jnp.float32)
            bias = []
            for j in range(MAXB):
                live = table_ref[0, 2 * ROW + i * MAXB + j]
                bias.append(jnp.where(lanes < live, 0.0, MASKED))
            scores = scores * (1.0 / math.sqrt(HEAD)) + jnp.concatenate(bias, axis=1)
            top = jnp.max(scores, axis=-1, keepdims=True)
            expo = jnp.exp(scores - top)
            inverse = 1.0 / jnp.sum(expo, axis=-1, keepdims=True)
            probs[i] = (expo * inverse).astype(jnp.bfloat16)
            return carry
        lax.fori_loop(0, ROW, body, 0)

    def back_copy(h, d, r):
        return pltpu.make_async_remote_copy(
            src_ref=outs[h].at[rows_at(lax.rem(me + d, ROW)), :],
            dst_ref=got.at[:, columns(r, h)],
            send_sem=os_.at[h, d], recv_sem=or_.at[h, d],
            device_id=row_dev(lax.rem(me + d, ROW)), device_id_type=MESH)

    def home_copy(h):
        return pltpu.make_async_copy(
            outs[h].at[rows_at(me), :], got.at[:, columns(me, h)], or_.at[h, 0])

    def mix(h):
        def one(i):
            value = window(vals[h], i)
            mixed = jnp.dot(probs[i], value, preferred_element_type=jnp.float32)
            live = table_ref[0, ROW + i]
            outs[h][rows_at(i), :] = jnp.where(slots < live, mixed, 0.0).astype(jnp.bfloat16)

        def body(d, carry):
            one(lax.rem(me + d, ROW))

            @pl.when(d > 1)
            def _():
                back_copy(h, d - 1, me).start()
            return carry
        lax.fori_loop(1, ROW, body, 0)
        one(me)
        back_copy(h, ROW - 1, me).start()

    own_valid = table_ref[0, ROW + me]

    def error(h, acc):
        def body(d, total):
            r = sender(d)
            diff = (nxt[:, columns(r, h)].astype(jnp.float32)
                    - got[:, columns(r, h)].astype(jnp.float32))
            diff = jnp.where(slots < own_valid, diff, 0.0)
            return total + jnp.sum((diff * diff).reshape(BLK // 8, 8, HEAD), axis=0)
        return lax.fori_loop(0, ROW, body, acc)

    def wait_back(h):
        home_copy(h).wait()

        def body(d, carry):
            back_copy(h, d, sender(d)).wait_recv()
            return carry
        lax.fori_loop(1, ROW, body, 0)

    for kind in (0, 3, 1, 4):
        forward(kind)
    wait_queries(0)
    wait_halo(0)
    score(0)
    wait_halo(3)
    mix(0)
    home_copy(0).start()
    for kind in (2, 5):
        forward(kind)
    wait_queries(1)
    wait_halo(1)
    score(1)
    wait_halo(4)
    mix(1)
    home_copy(1).start()
    wait_queries(2)
    wait_halo(2)
    score(2)
    wait_halo(5)
    mix(2)
    home_copy(2).start()
    latent.wait()
    acc = jnp.zeros(TILE, jnp.float32)
    for h in range(SHARE):
        wait_back(h)
        acc = error(h, acc)
    acc = acc * weight_ref[...]
    home = pltpu.make_async_copy(got, out_hbm.at[0], misc.at[1])
    home.start()

    def exchange(stage, buf, place, count, device):
        def copy(d, slot):
            return pltpu.make_async_remote_copy(
                src_ref=buf.at[slot], dst_ref=buf.at[slot],
                send_sem=rs.at[stage, d], recv_sem=rr.at[stage, d],
                device_id=device(d), device_id_type=MESH)
        for d in range(1, count):
            copy(d, place).start()
        for d in range(1, count):
            copy(d, lax.rem(place + count - d, count)).wait_recv()
        total = buf[0]
        for slot in range(1, count):
            total = total + buf[slot]
        for d in range(1, count):
            copy(d, place).wait_send()
        return total

    red_x[me] = acc

    def drain(d, carry):
        for kind in range(3 * SHARE):
            share_copy(kind, d, me).wait_send()
        for h in range(SHARE):
            back_copy(h, d, me).wait_send()
        return carry
    lax.fori_loop(1, ROW, drain, 0)

    def drain_halo(d, carry):
        for kind in range(2 * SHARE):
            for_halo(kind, sender(d), d, lambda copy: copy.wait_send())
        return carry
    lax.fori_loop(0, ROW, drain_halo, 0)

    acc = exchange(0, red_x, me, ROW, lambda d: row_dev(lax.rem(me + d, ROW)))
    if ng > 1:
        red_y[g] = acc
        acc = exchange(1, red_y, g, ng, g_dev)
    red_z[z] = acc
    acc = exchange(2, red_z, z, nz, z_dev)
    loss_ref[0, 0] = jnp.sum(acc)
    home.wait()


def solution(mesh):
    ng = mesh.shape["grp"]
    nz = mesh.shape["tok"] // ROW
    finer = Mesh(mesh.devices.reshape(nz, 4, 2, ng), ("z", "x", "c", "grp"))
    tok = ("z", "x", "c")
    big = P("grp", tok, None)
    small = P("grp", None)
    dma = pltpu.SemaphoreType.DMA
    wide = pltpu.VMEM((3 * ROW, BLK, HEAD), jnp.bfloat16)
    row = pltpu.VMEM((ROW * BLK, HEAD), jnp.bfloat16)
    whole = pltpu.VMEM((BLK, D), jnp.bfloat16)
    anywhere = pl.BlockSpec(memory_space=pl.ANY)
    scalars = pl.BlockSpec(memory_space=pltpu.SMEM)

    tile = pl.BlockSpec(memory_space=pltpu.VMEM)

    def on_device(queries, keys, values, latent, *rows):
        table, weight = pl.pallas_call(
            functools.partial(tables, (nz, ng)),
            out_shape=(jax.ShapeDtypeStruct((1, 128), jnp.int32),
                       jax.ShapeDtypeStruct(TILE, jnp.float32)),
            in_specs=[scalars] * 4, out_specs=(scalars, tile),
        )(*rows)
        out, loss = pl.pallas_call(
            functools.partial(kernel, (nz, ng)),
            out_shape=(jax.ShapeDtypeStruct((1, BLK, D), jnp.bfloat16),
                       jax.ShapeDtypeStruct((1, 1), jnp.float32)),
            in_specs=[anywhere] * 4 + [scalars, tile],
            out_specs=(anywhere, scalars),
            scratch_shapes=[wide] * 6 + [row] * 6 + [
                pltpu.VMEM((ROW, BLK, SPAN), jnp.bfloat16), whole, whole,
                pltpu.VMEM((ROW, 8, 128), jnp.float32), pltpu.VMEM((max(ng, 2), 8, 128), jnp.float32),
                pltpu.VMEM((nz, 8, 128), jnp.float32),
                dma((3 * SHARE, ROW)), dma((3 * SHARE, ROW)),
                dma((2 * SHARE, ROW)), dma((2 * SHARE, ROW)),
                dma((2 * SHARE, ROW)), dma((2 * SHARE, ROW)),
                dma((SHARE, ROW)), dma((SHARE, ROW)), dma((2,)),
                dma((3, 8)), dma((3, 8))],
            compiler_params=pltpu.CompilerParams(
                collective_id=0, has_side_effects=True, vmem_limit_bytes=40 << 20),
        )(queries, keys, values, latent, table, weight)
        return out, loss.reshape(())

    return jax.shard_map(
        on_device, mesh=finer, in_specs=(big,) * 4 + (small,) * 4,
        out_specs=(big, P()), check_vma=False)
```

```python
import functools
import math

import jax
import jax.numpy as jnp
from jax import lax
from jax.experimental import pallas as pl
from jax.experimental.pallas import tpu as pltpu
from jax.sharding import Mesh
from jax.sharding import PartitionSpec as P

D = 3072
HEADS = 24
HEAD = 128
BLK = 128
MAXB = 8
ROW = 8
SHARE = HEADS // ROW
SPAN = MAXB * BLK
MASKED = -1e30
TILE = (8, 128)
MESH = pl.DeviceIdType.MESH


def rows_at(block):
    return pl.ds(pl.multiple_of(block * BLK, BLK), BLK)


def kernel(sizes, q_hbm, k_hbm, v_hbm, next_hbm, clip_ref, valid_ref, group_ref, reward_ref,
           out_hbm, loss_ref, kb0, kb1, kb2, vb0, vb1, vb2, qb0, qb1, qb2, ob0, ob1, ob2,
           probs, got, nxt, first_ref, live_ref, red_xy, red_z,
           xs, xr, us, ur, ds_, dr, os_, or_, misc, rs, rr):
    nz, ng = sizes
    total_blocks = nz * ROW
    clips = clip_ref.shape[1]
    z, x, c, g = (lax.axis_index(a) for a in ("z", "x", "c", "grp"))
    me = x * 2 + c
    keys, vals, qrys, outs = (kb0, kb1, kb2), (vb0, vb1, vb2), (qb0, qb1, qb2), (ob0, ob1, ob2)

    def row_dev(r):
        return {"x": r // 2, "c": lax.rem(r, 2)}

    def z_dev(dz):
        return {"z": lax.rem(z + dz, nz)}

    def g_dev(dg):
        return {"grp": lax.rem(g + dg, ng)}

    def source(kind):
        return (k_hbm, v_hbm, q_hbm)[kind // SHARE]

    def landing(kind, s):
        h = kind % SHARE
        if kind < 2 * SHARE:
            return (keys, vals)[kind // SHARE][h].at[ROW + s]
        return qrys[h].at[rows_at(s), :]

    def columns(r, h):
        return pl.ds(pl.multiple_of((r * SHARE + h) * HEAD, HEAD), HEAD)

    def share_copy(kind, d, s):
        r = lax.rem(me + d, ROW)
        return pltpu.make_async_remote_copy(
            src_ref=source(kind).at[0, :, columns(r, kind % SHARE)],
            dst_ref=landing(kind, s),
            send_sem=xs.at[kind, d], recv_sem=xr.at[kind, d],
            device_id=row_dev(r), device_id_type=MESH)

    def own_copy(kind):
        return pltpu.make_async_copy(
            source(kind).at[0, :, columns(me, kind % SHARE)], landing(kind, me), xr.at[kind, 0])

    def send_share(kind):
        own_copy(kind).start()

        def body(d, carry):
            share_copy(kind, d, me).start()
            return carry
        lax.fori_loop(1, ROW, body, 0)

    def sender(d):
        return lax.rem(me + ROW - d, ROW)

    def halo_copy(kind, s, d, up, own):
        buf = (keys, vals)[kind // SHARE][kind % SHARE]
        return pltpu.make_async_remote_copy(
            src_ref=source(kind).at[0, :, columns(me, kind % SHARE)] if own else buf.at[ROW + s],
            dst_ref=buf.at[s if up else 2 * ROW + s],
            send_sem=(us if up else ds_).at[kind, d], recv_sem=(ur if up else dr).at[kind, d],
            device_id=z_dev(1 if up else nz - 1), device_id_type=MESH)

    def for_halo(kind, s, d, act, own=False):
        @pl.when(s != 0)
        def _():
            act(halo_copy(kind, s, d, True, own))

        @pl.when(s != ROW - 1)
        def _():
            act(halo_copy(kind, s, d, False, own))

    def forward_one(kind, t):
        d = 1 + lax.rem(t + 6 * (1 - c), ROW - 1)
        s = sender(d)
        share_copy(kind, d, s).wait_recv()
        for_halo(kind, s, d, lambda copy: copy.start())

    def forward(kind):
        def body(t, carry):
            forward_one(kind, t)
            return carry
        lax.fori_loop(0, ROW - 1, body, 0)

    def wait_halo(kind):
        own_copy(kind).wait()

        def body(d, carry):
            for_halo(kind, sender(d), d, lambda copy: copy.wait_recv())
            return carry
        lax.fori_loop(0, ROW, body, 0)

    def wait_queries(h):
        kind = 2 * SHARE + h
        own_copy(kind).wait()

        def body(d, carry):
            share_copy(kind, d, sender(d)).wait_recv()
            return carry
        lax.fori_loop(1, ROW, body, 0)

    barrier = pltpu.get_barrier_semaphore()
    near, far = ROW * ng, nz

    def near_dev(p):
        r = lax.rem(me + p // ng, ROW)
        return {"x": r // 2, "c": lax.rem(r, 2), "grp": lax.rem(g + lax.rem(p, ng), ng)}

    def greet(device):
        def body(p, carry):
            pl.semaphore_signal(barrier, inc=1, device_id=device(p), device_id_type=MESH)
            return carry
        return body
    lax.fori_loop(1, far, greet(z_dev), 0)
    lax.fori_loop(1, near, greet(near_dev), 0)
    pl.semaphore_wait(barrier, near + far - 2)

    order = (0, 3, 6, 1, 4, 7, 2, 5, 8)
    for kind in order[:2]:
        send_share(kind)
    for kind in (0, 3, 1, 4, 2, 5):
        for_halo(kind, me, 0, lambda copy: copy.start(), own=True)
    for kind in order[2:]:
        send_share(kind)
    latent = pltpu.make_async_copy(next_hbm.at[0], nxt, misc.at[0])
    latent.start()

    def clip_of(block):
        def body(i, carry):
            begin, start, count, own = carry
            size = clip_ref[0, i]
            inside = (block >= begin) & (block < begin + size)
            return (begin + size, jnp.where(inside, begin, start), jnp.where(inside, size, count),
                    jnp.where(inside, i, own))
        zero = jnp.int32(0)
        _, start, count, own = lax.fori_loop(0, clips, body, (zero, zero, zero, zero))
        return start, count, own

    def note(i, carry):
        start, count, _ = clip_of(z * ROW + i)
        first_ref[i] = jnp.clip(start - (z * ROW - ROW), 0, 2 * ROW)
        for j in range(MAXB):
            live = valid_ref[0, jnp.minimum(start + j, total_blocks - 1)]
            live_ref[i * MAXB + j] = jnp.where(j < count, live, 0)
        return carry
    lax.fori_loop(0, ROW, note, 0)

    own_block = z * ROW + me
    own_start, own_count, own_clip = clip_of(own_block)
    own_group = group_ref[0, own_clip]
    own_valid = valid_ref[0, own_block]

    def member(i, carry):
        total, count = carry
        same = group_ref[0, i] == own_group
        return (total + jnp.where(same, reward_ref[0, i], 0.0), count + jnp.where(same, 1.0, 0.0))
    total, count = lax.fori_loop(0, clips, member, (jnp.float32(0), jnp.float32(0)))
    tokens = jnp.int32(0)
    for j in range(MAXB):
        live = valid_ref[0, jnp.minimum(own_start + j, total_blocks - 1)]
        tokens = tokens + jnp.where(j < own_count, live, 0)
    mean = jnp.full(TILE, total) / jnp.full(TILE, jnp.maximum(count, 1.0))
    adv = jnp.full(TILE, reward_ref[0, own_clip]) - mean
    weight = adv / jnp.full(TILE, (2.0 * D) * tokens.astype(jnp.float32))

    lanes = lax.broadcasted_iota(jnp.int32, (1, BLK), 1)
    slots = lax.broadcasted_iota(jnp.int32, (BLK, HEAD), 0)

    def window(buf, i):
        first = first_ref[i]
        return jnp.concatenate([buf[first + j] for j in range(MAXB)], axis=0)

    def score(h):
        def one(i):
            query = qrys[h][rows_at(i), :]
            key = window(keys[h], i)
            scores = lax.dot_general(query, key, (((1,), (1,)), ((), ())),
                                     preferred_element_type=jnp.float32)
            bias = []
            for j in range(MAXB):
                live = live_ref[i * MAXB + j]
                bias.append(jnp.where(lanes < live, 0.0, MASKED))
            scores = scores * (1.0 / math.sqrt(HEAD)) + jnp.concatenate(bias, axis=1)
            top = jnp.max(scores, axis=-1, keepdims=True)
            expo = jnp.exp(scores - top)
            inverse = 1.0 / jnp.sum(expo, axis=-1, keepdims=True)
            return (expo * inverse).astype(jnp.bfloat16)

        def body(n, carry):
            if h + 1 < SHARE:
                forward_one(h + 1, 2 * n)

                @pl.when(n < ROW // 2 - 1)
                def _():
                    forward_one(h + 1, 2 * n + 1)
            first, second = one(2 * n), one(2 * n + 1)
            probs[2 * n] = first
            probs[2 * n + 1] = second
            return carry
        lax.fori_loop(0, ROW // 2, body, 0)

    def back_copy(h, d, r):
        return pltpu.make_async_remote_copy(
            src_ref=outs[h].at[rows_at(lax.rem(me + d, ROW)), :],
            dst_ref=got.at[:, columns(r, h)],
            send_sem=os_.at[h, d], recv_sem=or_.at[h, d],
            device_id=row_dev(lax.rem(me + d, ROW)), device_id_type=MESH)

    def home_copy(h):
        return pltpu.make_async_copy(
            outs[h].at[rows_at(me), :], got.at[:, columns(me, h)], or_.at[h, 0])

    def mix(h):
        def one(i):
            value = window(vals[h], i)
            mixed = jnp.dot(probs[i], value, preferred_element_type=jnp.float32)
            live = valid_ref[0, z * ROW + i]
            outs[h][rows_at(i), :] = jnp.where(slots < live, mixed, 0.0).astype(jnp.bfloat16)

        def body(d, carry):
            one(lax.rem(me + d, ROW))

            @pl.when(d > 1)
            def _():
                back_copy(h, d - 1, me).start()
            if h + 1 < SHARE:
                forward_one(SHARE + h + 1, d - 1)
            return carry
        lax.fori_loop(1, ROW, body, 0)
        one(me)
        back_copy(h, ROW - 1, me).start()

    def error(h, acc):
        def body(d, total):
            r = sender(d)
            diff = (nxt[:, columns(r, h)].astype(jnp.float32)
                    - got[:, columns(r, h)].astype(jnp.float32))
            diff = jnp.where(slots < own_valid, diff, 0.0)
            return total + jnp.sum((diff * diff).reshape(BLK // 8, 8, HEAD), axis=0)
        return lax.fori_loop(0, ROW, body, acc)

    def wait_back(h):
        home_copy(h).wait()

        def body(d, carry):
            back_copy(h, d, sender(d)).wait_recv()
            return carry
        lax.fori_loop(1, ROW, body, 0)

    forward(0)
    forward(SHARE)
    for h in range(SHARE):
        wait_queries(h)
        wait_halo(h)
        score(h)
        wait_halo(SHARE + h)
        mix(h)
        home_copy(h).start()
    latent.wait()
    acc = jnp.zeros(TILE, jnp.float32)
    for h in range(SHARE):
        wait_back(h)
        acc = error(h, acc)

    def exchange(buf, stage, place, other, count, device, between):
        def copy(p, slot):
            return pltpu.make_async_remote_copy(
                src_ref=buf.at[slot], dst_ref=buf.at[slot],
                send_sem=rs.at[stage, p], recv_sem=rr.at[stage, p],
                device_id=device(p), device_id_type=MESH)

        def start(p, carry):
            copy(p, place).start()
            return carry

        def land(p, carry):
            copy(p, other(p)).wait_recv()
            return carry

        def sent(p, carry):
            copy(p, place).wait_send()
            return carry
        lax.fori_loop(1, count, start, 0)
        between()
        lax.fori_loop(1, count, land, 0)
        total = jnp.sum(buf[...], axis=0)
        return total, lambda: lax.fori_loop(1, count, sent, 0)

    def drain(d, carry):
        for kind in range(3 * SHARE):
            share_copy(kind, d, me).wait_send()
        for h in range(SHARE):
            back_copy(h, d, me).wait_send()
        return carry

    def drain_halo(d, carry):
        for kind in range(2 * SHARE):
            for_halo(kind, sender(d), d, lambda copy: copy.wait_send())
        return carry

    red_xy[me * ng + g] = jnp.sum(acc, axis=0, keepdims=True) * weight[:1]
    home = pltpu.make_async_copy(got, out_hbm.at[0], misc.at[1])
    home.start()
    acc, sent_near = exchange(
        red_xy, 0, me * ng + g,
        lambda p: lax.rem(me + ROW - p // ng, ROW) * ng + lax.rem(g + ng - lax.rem(p, ng), ng),
        near, near_dev, lambda: lax.fori_loop(1, ROW, drain, 0))
    red_z[z] = acc
    acc, sent_far = exchange(
        red_z, 1, z, lambda p: lax.rem(z + nz - p, nz), far, z_dev,
        lambda: lax.fori_loop(0, ROW, drain_halo, 0))
    loss_ref[0, 0] = jnp.sum(acc)
    sent_near()
    sent_far()
    home.wait()


def solution(mesh):
    ng = mesh.shape["grp"]
    nz = mesh.shape["tok"] // ROW
    finer = Mesh(mesh.devices.reshape(nz, 4, 2, ng), ("z", "x", "c", "grp"))
    tok = ("z", "x", "c")
    big = P("grp", tok, None)
    small = P("grp", None)
    dma = pltpu.SemaphoreType.DMA
    wide = pltpu.VMEM((3 * ROW, BLK, HEAD), jnp.bfloat16)
    row = pltpu.VMEM((ROW * BLK, HEAD), jnp.bfloat16)
    whole = pltpu.VMEM((BLK, D), jnp.bfloat16)
    anywhere = pl.BlockSpec(memory_space=pl.ANY)
    scalars = pl.BlockSpec(memory_space=pltpu.SMEM)


    def on_device(*args):
        out, loss = pl.pallas_call(
            functools.partial(kernel, (nz, ng)),
            out_shape=(jax.ShapeDtypeStruct((1, BLK, D), jnp.bfloat16),
                       jax.ShapeDtypeStruct((1, 1), jnp.float32)),
            in_specs=[anywhere] * 4 + [scalars] * 4,
            out_specs=(anywhere, scalars),
            scratch_shapes=[wide] * 6 + [row] * 6 + [
                pltpu.VMEM((ROW, BLK, SPAN), jnp.bfloat16), whole, whole,
                pltpu.SMEM((ROW,), jnp.int32), pltpu.SMEM((ROW * MAXB,), jnp.int32),
                pltpu.VMEM((ROW * ng, 1, 128), jnp.float32), pltpu.VMEM((nz, 1, 128), jnp.float32),
                dma((3 * SHARE, ROW)), dma((3 * SHARE, ROW)),
                dma((2 * SHARE, ROW)), dma((2 * SHARE, ROW)),
                dma((2 * SHARE, ROW)), dma((2 * SHARE, ROW)),
                dma((SHARE, ROW)), dma((SHARE, ROW)), dma((2,)),
                dma((2, ROW * ng)), dma((2, ROW * ng))],
            compiler_params=pltpu.CompilerParams(
                collective_id=0, has_side_effects=True),
        )(*args)
        return out, loss.reshape(())

    return jax.shard_map(
        on_device, mesh=finer, in_specs=(big,) * 4 + (small,) * 4,
        out_specs=(big, P()), check_vma=False)
```

```python
import functools
import math

import jax
import jax.numpy as jnp
from jax import lax
from jax.experimental import pallas as pl
from jax.experimental.pallas import tpu as pltpu
from jax.sharding import Mesh
from jax.sharding import PartitionSpec as P

D = 3072
HEADS = 24
HEAD = 128
BLK = 128
MAXB = 8
ROW = 8
SHARE = HEADS // ROW
SPAN = MAXB * BLK
MASKED = -1e30
TILE = (8, 128)
LAST = 3 * SHARE
MESH = pl.DeviceIdType.MESH


def rows_at(block):
    return pl.ds(pl.multiple_of(block * BLK, BLK), BLK)


def kernel(sizes, q_hbm, k_hbm, v_hbm, next_hbm, clip_ref, valid_ref, group_ref, reward_ref,
           out_hbm, loss_ref, kb0, kb1, kb2, vb0, vb1, vb2, qb0, qb1, qb2, ob0, ob1, ob2, nb,
           probs, got, nxt, weights, first_ref, live_ref, red_zg, red_x,
           xs, xr, us, ur, ds_, dr, os_, or_, misc, rs, rr, word):
    nz, ng = sizes
    total_blocks = nz * ROW
    clips = clip_ref.shape[1]
    z, x, c, g = (lax.axis_index(a) for a in ("z", "x", "c", "grp"))
    me = x * 2 + c
    keys, vals, qrys, outs = (kb0, kb1, kb2), (vb0, vb1, vb2), (qb0, qb1, qb2), (ob0, ob1, ob2)

    def row_dev(r):
        return {"x": r // 2, "c": lax.rem(r, 2)}

    def z_dev(dz):
        return {"z": lax.rem(z + dz, nz)}

    def g_dev(dg):
        return {"grp": lax.rem(g + dg, ng)}

    def source(kind):
        return (k_hbm, v_hbm, q_hbm, next_hbm)[kind // SHARE]

    def landing(kind, s):
        h = head_of(kind)
        if kind == LAST:
            return nb.at[rows_at(s), :]
        if kind < 2 * SHARE:
            return (keys, vals)[kind // SHARE][h].at[ROW + s]
        return qrys[h].at[rows_at(s), :]

    def head_of(kind):
        return SHARE - 1 if kind == LAST else kind % SHARE

    def columns(r, h):
        return pl.ds(pl.multiple_of((r * SHARE + h) * HEAD, HEAD), HEAD)

    def share_copy(kind, d, s):
        r = lax.rem(me + d, ROW)
        return pltpu.make_async_remote_copy(
            src_ref=source(kind).at[0, :, columns(r, head_of(kind))],
            dst_ref=landing(kind, s),
            send_sem=xs.at[kind, d], recv_sem=xr.at[kind, d],
            device_id=row_dev(r), device_id_type=MESH)

    def own_copy(kind):
        return pltpu.make_async_copy(
            source(kind).at[0, :, columns(me, head_of(kind))], landing(kind, me), xr.at[kind, 0])

    def nth(t):
        return 1 + lax.rem(t + 6 * c, ROW - 1)

    def send_share(kind):
        def body(t, carry):
            share_copy(kind, nth(t), me).start()
            return carry
        lax.fori_loop(1, ROW - 1, body, 0)

    def sender(d):
        return lax.rem(me + ROW - d, ROW)

    def halo_copy(kind, s, d, up, own):
        buf = (keys, vals)[kind // SHARE][kind % SHARE]
        return pltpu.make_async_remote_copy(
            src_ref=source(kind).at[0, :, columns(me, kind % SHARE)] if own else buf.at[ROW + s],
            dst_ref=buf.at[s if up else 2 * ROW + s],
            send_sem=(us if up else ds_).at[kind, d], recv_sem=(ur if up else dr).at[kind, d],
            device_id=z_dev(1 if up else nz - 1), device_id_type=MESH)

    def for_halo(kind, s, d, act, own=False):
        @pl.when(s != 0)
        def _():
            act(halo_copy(kind, s, d, True, own))

        @pl.when(s != ROW - 1)
        def _():
            act(halo_copy(kind, s, d, False, own))

    def rnth(t):
        return 1 + lax.rem(t + 6 * (1 - c), ROW - 1)

    def forward_one(kind, t):
        d = rnth(t)
        s = sender(d)
        share_copy(kind, d, s).wait_recv()
        for_halo(kind, s, d, lambda copy: copy.start())

    def forward(kind):
        def body(t, carry):
            forward_one(kind, t)
            return carry
        lax.fori_loop(1, ROW - 1, body, 0)

    def wait_halo(kind):
        own_copy(kind).wait()

        def body(d, carry):
            for_halo(kind, sender(d), d, lambda copy: copy.wait_recv())
            return carry
        lax.fori_loop(0, ROW, body, 0)

    def wait_share(kind):
        own_copy(kind).wait()

        def body(d, carry):
            share_copy(kind, d, sender(d)).wait_recv()
            return carry
        lax.fori_loop(1, ROW, body, 0)

    barrier = pltpu.get_barrier_semaphore()
    across = [z_dev(1), z_dev(nz - 1), g_dev(1), g_dev(ng - 1)]

    def greet(d, carry):
        pl.semaphore_signal(barrier, inc=1, device_id=row_dev(lax.rem(me + d, ROW)), device_id_type=MESH)
        return carry
    for device in across:
        pl.semaphore_signal(barrier, inc=1, device_id=device, device_id_type=MESH)
    lax.fori_loop(1, ROW, greet, 0)
    pl.semaphore_wait(barrier, ROW - 1 + len(across))

    def tell(n, devices):
        for device in devices:
            pl.semaphore_signal(word.at[n], inc=1, device_id=device, device_id_type=MESH)

    hops = nz // 2
    tell(0, across)

    order = (0, 3, 6, 1, 4, 7, 2, 5, 8, LAST)
    streams = (0, 3, 1, 4, 2, 5)
    for kind in order:
        share_copy(kind, nth(0), me).start()
    for kind in order[:2]:
        send_share(kind)
    for kind in streams:
        for_halo(kind, me, 0, lambda copy: copy.start(), own=True)
    for kind in streams:
        forward_one(kind, 0)
    for kind in order[2:]:
        send_share(kind)
    for kind in order:
        own_copy(kind).start()
    latent = pltpu.make_async_copy(next_hbm.at[0], nxt, misc.at[0])
    latent.start()

    def clip_of(block):
        def body(i, carry):
            begin, start, count, own = carry
            size = clip_ref[0, i]
            inside = (block >= begin) & (block < begin + size)
            return (begin + size, jnp.where(inside, begin, start), jnp.where(inside, size, count),
                    jnp.where(inside, i, own))
        zero = jnp.int32(0)
        _, start, count, own = lax.fori_loop(0, clips, body, (zero, zero, zero, zero))
        return start, count, own

    def note(i, carry):
        start, count, _ = clip_of(z * ROW + i)
        first_ref[i] = jnp.clip(start - (z * ROW - ROW), 0, 2 * ROW)
        for j in range(MAXB):
            live = valid_ref[0, jnp.minimum(start + j, total_blocks - 1)]
            live_ref[i * MAXB + j] = jnp.where(j < count, live, 0)
        return carry
    lax.fori_loop(0, ROW, note, 0)

    def weigh(b, carry):
        start, count, own = clip_of(z * ROW + b)
        group = group_ref[0, own]

        def member(i, sums):
            total, number = sums
            same = group_ref[0, i] == group
            return (total + jnp.where(same, reward_ref[0, i], 0.0), number + jnp.where(same, 1.0, 0.0))
        total, number = lax.fori_loop(0, clips, member, (jnp.float32(0), jnp.float32(0)))
        tokens = jnp.int32(0)
        for j in range(MAXB):
            tokens = tokens + live_ref[b * MAXB + j]
        mean = jnp.full(TILE, total) / jnp.full(TILE, jnp.maximum(number, 1.0))
        adv = jnp.full(TILE, reward_ref[0, own]) - mean
        weights[b] = adv / jnp.full(TILE, (2.0 * D) * tokens.astype(jnp.float32))
        return carry

    own_valid = valid_ref[0, z * ROW + me]
    lanes = lax.broadcasted_iota(jnp.int32, (1, BLK), 1)
    slots = lax.broadcasted_iota(jnp.int32, (BLK, HEAD), 0)

    def window(buf, i):
        first = first_ref[i]
        return jnp.concatenate([buf[first + j] for j in range(MAXB)], axis=0)

    def score(h):
        def one(i):
            query = qrys[h][rows_at(i), :]
            key = window(keys[h], i)
            scores = lax.dot_general(query, key, (((1,), (1,)), ((), ())),
                                     preferred_element_type=jnp.float32)
            bias = []
            for j in range(MAXB):
                live = live_ref[i * MAXB + j]
                bias.append(jnp.where(lanes < live, 0.0, MASKED))
            scores = scores * (1.0 / math.sqrt(HEAD)) + jnp.concatenate(bias, axis=1)
            top = jnp.max(scores, axis=-1, keepdims=True)
            expo = jnp.exp(scores - top)
            inverse = 1.0 / jnp.sum(expo, axis=-1, keepdims=True)
            return (expo * inverse).astype(jnp.bfloat16)

        def body(n, carry):
            if h + 1 < SHARE:
                @pl.when(n < ROW // 2 - 1)
                def _():
                    forward_one(h + 1, 2 * n + 1)
                    forward_one(h + 1, 2 * n + 2)
            first, second = one(2 * n), one(2 * n + 1)
            probs[2 * n] = first
            probs[2 * n + 1] = second
            return carry
        lax.fori_loop(0, ROW // 2, body, 0)

    def back_copy(h, d, r):
        return pltpu.make_async_remote_copy(
            src_ref=outs[h].at[rows_at(lax.rem(me + d, ROW)), :],
            dst_ref=got.at[:, columns(r, h)],
            send_sem=os_.at[h, d], recv_sem=or_.at[h, d],
            device_id=row_dev(lax.rem(me + d, ROW)), device_id_type=MESH)

    def home_copy(h):
        return pltpu.make_async_copy(
            outs[h].at[rows_at(me), :], got.at[:, columns(me, h)], or_.at[h, 0])

    def squares(latent_block, velocity_block, live):
        diff = latent_block.astype(jnp.float32) - velocity_block.astype(jnp.float32)
        diff = jnp.where(slots < live, diff, 0.0)
        return jnp.sum((diff * diff).reshape(BLK // 8, 8, HEAD), axis=0)

    def mix(h, total):
        def one(i):
            mixed = jnp.dot(probs[i], window(vals[h], i), preferred_element_type=jnp.float32)
            live = valid_ref[0, z * ROW + i]
            mixed = jnp.where(slots < live, mixed, 0.0).astype(jnp.bfloat16)
            if h < SHARE - 1:
                return mixed, 0.0
            return mixed, squares(nb[rows_at(i), :], mixed, live) * weights[i]

        def pair(d, e, total):
            first, second = lax.rem(me + d, ROW), lax.rem(me + e, ROW)
            (one_first, err_first), (one_second, err_second) = one(first), one(second)
            outs[h][rows_at(first), :] = one_first
            outs[h][rows_at(second), :] = one_second
            return total + err_first + err_second

        def body(n, total):
            total = pair(2 * n + 2, 2 * n + 3, total)

            @pl.when(n > 0)
            def _():
                back_copy(h, 2 * n, me).start()
                back_copy(h, 2 * n + 1, me).start()
            if h + 1 < SHARE:
                forward_one(SHARE + h + 1, 2 * n + 1)
                forward_one(SHARE + h + 1, 2 * n + 2)
            return total
        total = lax.fori_loop(0, ROW // 2 - 1, body, total)
        total = pair(1, 0, total)
        for d in (ROW - 2, ROW - 1, 1):
            back_copy(h, d, me).start()
        return total

    def error(h):
        def body(d, total):
            r = sender(d)
            return total + squares(nxt[:, columns(r, h)], got[:, columns(r, h)], own_valid)
        return lax.fori_loop(0, ROW, body, jnp.zeros(TILE, jnp.float32)) * weights[me]

    def wait_back(h):
        home_copy(h).wait()

        def body(d, carry):
            back_copy(h, d, sender(d)).wait_recv()
            return carry
        lax.fori_loop(1, ROW, body, 0)

    forward(0)
    pl.semaphore_wait(word.at[0], len(across))
    tell(1, across[:2])
    forward(SHARE)
    for n in range(1, hops - 1):
        pl.semaphore_wait(word.at[n], 2)
        tell(n + 1, across[:2] if n < hops - 2 else [g_dev(d) for d in range(1, ng)])
    acc = jnp.zeros(TILE, jnp.float32)
    for h in range(SHARE):
        wait_share(2 * SHARE + h)
        if h == 1:
            lax.fori_loop(0, ROW, weigh, 0)
        if h == SHARE - 1:
            wait_share(LAST)
        wait_halo(h)
        score(h)
        wait_halo(SHARE + h)
        if h == SHARE - 1:
            latent.wait()
            for e in range(SHARE - 1):
                wait_back(e)
                acc = acc + error(e)
        acc = mix(h, acc)
        home_copy(h).start()
    pl.semaphore_wait(word.at[hops - 1], ng - 1)

    def exchange(buf, stage, place, other, count, device, between):
        def copy(p, slot):
            return pltpu.make_async_remote_copy(
                src_ref=buf.at[slot], dst_ref=buf.at[slot],
                send_sem=rs.at[stage, p], recv_sem=rr.at[stage, p],
                device_id=device(p), device_id_type=MESH)

        def start(p, carry):
            copy(1 + lax.rem(p + count // 2 - 2, count - 1), place).start()
            return carry

        def land(p, carry):
            copy(p, other(p)).wait_recv()
            return carry

        def sent(p, carry):
            copy(p, place).wait_send()
            return carry
        lax.fori_loop(1, count, start, 0)
        between()
        lax.fori_loop(1, count, land, 0)
        total = jnp.sum(buf[...], axis=0)
        return total, lambda: lax.fori_loop(1, count, sent, 0)

    def drain(d, carry):
        for kind in range(3 * SHARE + 1):
            share_copy(kind, d, me).wait_send()
        for h in range(SHARE):
            back_copy(h, d, me).wait_send()
        return carry

    def drain_halo(d, carry):
        for kind in range(2 * SHARE):
            for_halo(kind, sender(d), d, lambda copy: copy.wait_send())
        return carry

    red_zg[z * ng + g] = jnp.sum(acc, axis=0, keepdims=True)
    home = pltpu.make_async_copy(got, out_hbm.at[0], misc.at[1])

    def rest():
        wait_back(SHARE - 1)
        home.start()
        lax.fori_loop(1, ROW, drain, 0)

    def plane_dev(p):
        return {"z": lax.rem(z + p // ng, nz), "grp": lax.rem(g + lax.rem(p, ng), ng)}

    acc, sent_plane = exchange(
        red_zg, 0, z * ng + g,
        lambda p: lax.rem(z + nz - p // ng, nz) * ng + lax.rem(g + ng - lax.rem(p, ng), ng),
        nz * ng, plane_dev, rest)
    red_x[me] = acc
    acc, sent_row = exchange(
        red_x, 1, me, lambda p: lax.rem(me + ROW - p, ROW), ROW, lambda p: row_dev(lax.rem(me + p, ROW)),
        lambda: lax.fori_loop(0, ROW, drain_halo, 0))
    loss_ref[0, 0] = jnp.sum(acc)
    sent_plane()
    sent_row()
    home.wait()


def solution(mesh):
    ng = mesh.shape["grp"]
    nz = mesh.shape["tok"] // ROW
    finer = Mesh(mesh.devices.reshape(nz, 4, 2, ng), ("z", "x", "c", "grp"))
    tok = ("z", "x", "c")
    big = P("grp", tok, None)
    small = P("grp", None)
    dma = pltpu.SemaphoreType.DMA
    wide = pltpu.VMEM((3 * ROW, BLK, HEAD), jnp.bfloat16)
    row = pltpu.VMEM((ROW * BLK, HEAD), jnp.bfloat16)
    whole = pltpu.VMEM((BLK, D), jnp.bfloat16)
    anywhere = pl.BlockSpec(memory_space=pl.ANY)
    scalars = pl.BlockSpec(memory_space=pltpu.SMEM)


    def on_device(*args):
        out, loss = pl.pallas_call(
            functools.partial(kernel, (nz, ng)),
            out_shape=(jax.ShapeDtypeStruct((1, BLK, D), jnp.bfloat16),
                       jax.ShapeDtypeStruct((1, 1), jnp.float32)),
            in_specs=[anywhere] * 4 + [scalars] * 4,
            out_specs=(anywhere, scalars),
            scratch_shapes=[wide] * 6 + [row] * 7 + [
                pltpu.VMEM((ROW, BLK, SPAN), jnp.bfloat16), whole, whole,
                pltpu.VMEM((ROW, 8, 128), jnp.float32),
                pltpu.SMEM((ROW,), jnp.int32), pltpu.SMEM((ROW * MAXB,), jnp.int32),
                pltpu.VMEM((nz * ng, 1, 128), jnp.float32), pltpu.VMEM((ROW, 1, 128), jnp.float32),
                dma((3 * SHARE + 1, ROW)), dma((3 * SHARE + 1, ROW)),
                dma((2 * SHARE, ROW)), dma((2 * SHARE, ROW)),
                dma((2 * SHARE, ROW)), dma((2 * SHARE, ROW)),
                dma((SHARE, ROW)), dma((SHARE, ROW)), dma((2,)),
                dma((2, nz * ng)), dma((2, nz * ng)),
                pltpu.SemaphoreType.REGULAR((nz // 2,))],
            compiler_params=pltpu.CompilerParams(
                collective_id=0, has_side_effects=True),
        )(*args)
        return out, loss.reshape(())

    return jax.shard_map(
        on_device, mesh=finer, in_specs=(big,) * 4 + (small,) * 4,
        out_specs=(big, P()), check_vma=False)
```

```python
import functools
import math

import jax
import jax.numpy as jnp
from jax import lax
from jax.experimental import pallas as pl
from jax.experimental.pallas import tpu as pltpu
from jax.sharding import Mesh
from jax.sharding import PartitionSpec as P

D = 3072
HEADS = 24
HEAD = 128
BLK = 128
MAXB = 8
ROW = 8
SHARE = HEADS // ROW
SPAN = MAXB * BLK
MASKED = -1e30
TILE = (8, 128)
LAST = 3 * SHARE
MESH = pl.DeviceIdType.MESH


def rows_at(block):
    return pl.ds(pl.multiple_of(block * BLK, BLK), BLK)


def kernel(sizes, q_hbm, k_hbm, v_hbm, next_hbm, clip_ref, valid_ref, group_ref, reward_ref,
           out_hbm, loss_ref, kb0, kb1, kb2, vb0, vb1, vb2, qb0, qb1, qb2, ob0, ob1, ob2, nb,
           probs, got, nxt, weights, first_ref, live_ref, red_zg, red_x,
           xs, xr, qr, own, zs, zr, os_, or_, misc, rs, rr, word):
    nz, ng = sizes
    total_blocks = nz * ROW
    clips = clip_ref.shape[1]
    z, x, c, g = (lax.axis_index(a) for a in ("z", "x", "c", "grp"))
    me = x * 2 + c
    keys, vals, qrys, outs = (kb0, kb1, kb2), (vb0, vb1, vb2), (qb0, qb1, qb2), (ob0, ob1, ob2)

    def row_dev(r):
        return {"x": r // 2, "c": lax.rem(r, 2)}

    def z_dev(dz):
        return {"z": lax.rem(z + dz, nz)}

    def g_dev(dg):
        return {"grp": lax.rem(g + dg, ng)}

    def source(kind):
        return (k_hbm, v_hbm, q_hbm, next_hbm)[kind // SHARE]

    def landing(kind, s):
        h = head_of(kind)
        if kind == LAST:
            return nb.at[rows_at(s), :]
        if kind < 2 * SHARE:
            return (keys, vals)[kind // SHARE][h].at[ROW + s]
        return qrys[h].at[rows_at(s), :]

    def head_of(kind):
        return SHARE - 1 if kind == LAST else kind % SHARE

    def columns(r, h):
        return pl.ds(pl.multiple_of((r * SHARE + h) * HEAD, HEAD), HEAD)

    def share_copy(kind, d, s):
        r = lax.rem(me + d, ROW)
        return pltpu.make_async_remote_copy(
            src_ref=source(kind).at[0, :, columns(r, head_of(kind))],
            dst_ref=landing(kind, s),
            send_sem=xs.at[kind], recv_sem=xr.at[kind, d] if kind < 2 * SHARE else qr.at[kind - 2 * SHARE],
            device_id=row_dev(r), device_id_type=MESH)

    def whole_share(kind):
        part = qb0.at[pl.ds(0, (ROW - 1) * BLK), :]
        return pltpu.make_async_remote_copy(
            src_ref=part, dst_ref=part, send_sem=xs.at[kind], recv_sem=qr.at[max(kind - 2 * SHARE, 0)],
            device_id=row_dev(lax.rem(me + 1, ROW)), device_id_type=MESH)

    def own_copy(kind):
        return pltpu.make_async_copy(
            source(kind).at[0, :, columns(me, head_of(kind))], landing(kind, me), own.at[kind])

    def nth(t):
        return 1 + lax.rem(t + 6 * c, ROW - 1)

    def send_share(kind):
        def body(t, carry):
            share_copy(kind, nth(t), me).start()
            return carry
        lax.fori_loop(1, ROW - 1, body, 0)

    def sender(d):
        return lax.rem(me + ROW - d, ROW)

    def halo_copy(kind, s, d, up, own):
        buf = (keys, vals)[kind // SHARE][kind % SHARE]
        return pltpu.make_async_remote_copy(
            src_ref=source(kind).at[0, :, columns(me, kind % SHARE)] if own else buf.at[ROW + s],
            dst_ref=buf.at[s if up else 2 * ROW + s],
            send_sem=zs.at[kind], recv_sem=zr.at[kind, 0 if up else 1],
            device_id=z_dev(1 if up else nz - 1), device_id_type=MESH)

    def for_halo(kind, s, d, act, own=False):
        @pl.when(s != 0)
        def _():
            act(halo_copy(kind, s, d, True, own))

        @pl.when(s != ROW - 1)
        def _():
            act(halo_copy(kind, s, d, False, own))

    def rnth(t):
        return 1 + lax.rem(t + 6 * (1 - c), ROW - 1)

    def forward_one(kind, t):
        d = rnth(t)
        s = sender(d)
        share_copy(kind, d, s).wait_recv()
        for_halo(kind, s, d, lambda copy: copy.start())

    def forward(kind):
        def body(t, carry):
            forward_one(kind, t)
            return carry
        lax.fori_loop(1, ROW - 1, body, 0)

    def whole_halo(kind, up):
        buf = (keys, vals)[kind // SHARE][kind % SHARE]
        both = buf.at[pl.ds(0, 2 * (ROW - 1))]
        side = buf.at[pl.ds(1 if up else 2 * ROW, ROW - 1)]
        return pltpu.make_async_remote_copy(
            src_ref=both, dst_ref=side, send_sem=zs.at[kind], recv_sem=zr.at[kind, 0 if up else 1],
            device_id=z_dev(1 if up else nz - 1), device_id_type=MESH)

    def wait_halo(kind):
        own_copy(kind).wait()
        whole_halo(kind, True).wait_recv()
        whole_halo(kind, False).wait_recv()

    def wait_share(kind):
        own_copy(kind).wait()
        whole_share(kind).wait_recv()

    barrier = pltpu.get_barrier_semaphore()
    across = [z_dev(1), z_dev(nz - 1), g_dev(1), g_dev(ng - 1)]

    def greet(d, carry):
        pl.semaphore_signal(barrier, inc=1, device_id=row_dev(lax.rem(me + d, ROW)), device_id_type=MESH)
        return carry
    for device in across:
        pl.semaphore_signal(barrier, inc=1, device_id=device, device_id_type=MESH)
    lax.fori_loop(1, ROW, greet, 0)
    pl.semaphore_wait(barrier, ROW - 1 + len(across))

    def tell(n, devices):
        for device in devices:
            pl.semaphore_signal(word.at[n], inc=1, device_id=device, device_id_type=MESH)

    hops = nz // 2
    tell(0, across)

    order = (0, 3, 6, 1, 4, 7, 2, 5, 8, LAST)
    streams = (0, 3, 1, 4, 2, 5)
    for kind in order:
        share_copy(kind, nth(0), me).start()
    for kind in order[:2]:
        send_share(kind)
    for kind in streams:
        for_halo(kind, me, 0, lambda copy: copy.start(), own=True)
    for kind in streams:
        forward_one(kind, 0)
    for kind in order[2:]:
        send_share(kind)
    for kind in order:
        own_copy(kind).start()
    latent = pltpu.make_async_copy(next_hbm.at[0], nxt, misc.at[0])
    latent.start()

    def clip_of(block):
        def body(i, carry):
            begin, start, count, own = carry
            size = clip_ref[0, i]
            inside = (block >= begin) & (block < begin + size)
            return (begin + size, jnp.where(inside, begin, start), jnp.where(inside, size, count),
                    jnp.where(inside, i, own))
        zero = jnp.int32(0)
        _, start, count, own = lax.fori_loop(0, clips, body, (zero, zero, zero, zero))
        return start, count, own

    def note(i, carry):
        start, count, _ = clip_of(z * ROW + i)
        first_ref[i] = jnp.clip(start - (z * ROW - ROW), 0, 2 * ROW)
        for j in range(MAXB):
            live = valid_ref[0, jnp.minimum(start + j, total_blocks - 1)]
            live_ref[i * MAXB + j] = jnp.where(j < count, live, 0)
        return carry
    lax.fori_loop(0, ROW, note, 0)

    def weigh(b, carry):
        start, count, own = clip_of(z * ROW + b)
        group = group_ref[0, own]

        def member(i, sums):
            total, number = sums
            same = group_ref[0, i] == group
            return (total + jnp.where(same, reward_ref[0, i], 0.0), number + jnp.where(same, 1.0, 0.0))
        total, number = lax.fori_loop(0, clips, member, (jnp.float32(0), jnp.float32(0)))
        tokens = jnp.int32(0)
        for j in range(MAXB):
            tokens = tokens + live_ref[b * MAXB + j]
        mean = jnp.full(TILE, total) / jnp.full(TILE, jnp.maximum(number, 1.0))
        adv = jnp.full(TILE, reward_ref[0, own]) - mean
        weights[b] = adv / jnp.full(TILE, (2.0 * D) * tokens.astype(jnp.float32))
        return carry

    own_valid = valid_ref[0, z * ROW + me]
    lanes = lax.broadcasted_iota(jnp.int32, (1, BLK), 1)
    slots = lax.broadcasted_iota(jnp.int32, (BLK, HEAD), 0)

    def window(buf, i):
        first = first_ref[i]
        return jnp.concatenate([buf[first + j] for j in range(MAXB)], axis=0)

    def score(h):
        def one(i):
            query = qrys[h][rows_at(i), :]
            key = window(keys[h], i)
            scores = lax.dot_general(query, key, (((1,), (1,)), ((), ())),
                                     preferred_element_type=jnp.float32)
            bias = []
            for j in range(MAXB):
                live = live_ref[i * MAXB + j]
                bias.append(jnp.where(lanes < live, 0.0, MASKED))
            scores = scores * (1.0 / math.sqrt(HEAD)) + jnp.concatenate(bias, axis=1)
            top = jnp.max(scores, axis=-1, keepdims=True)
            expo = jnp.exp(scores - top)
            inverse = 1.0 / jnp.sum(expo, axis=-1, keepdims=True)
            return (expo * inverse).astype(jnp.bfloat16)

        def body(n, carry):
            if h + 1 < SHARE:
                @pl.when(n < ROW // 2 - 1)
                def _():
                    forward_one(h + 1, 2 * n + 1)
                    forward_one(h + 1, 2 * n + 2)
            first, second = one(2 * n), one(2 * n + 1)
            probs[2 * n] = first
            probs[2 * n + 1] = second
            return carry
        lax.fori_loop(0, ROW // 2, body, 0)

    def back_copy(h, d, r):
        return pltpu.make_async_remote_copy(
            src_ref=outs[h].at[rows_at(lax.rem(me + d, ROW)), :],
            dst_ref=got.at[:, columns(r, h)],
            send_sem=os_.at[h], recv_sem=or_.at[h],
            device_id=row_dev(lax.rem(me + d, ROW)), device_id_type=MESH)

    def home_copy(h):
        return pltpu.make_async_copy(
            outs[h].at[rows_at(me), :], got.at[:, columns(me, h)], own.at[LAST + 1 + h])

    def squares(latent_block, velocity_block, live):
        diff = latent_block.astype(jnp.float32) - velocity_block.astype(jnp.float32)
        diff = jnp.where(slots < live, diff, 0.0)
        return jnp.sum((diff * diff).reshape(BLK // 8, 8, HEAD), axis=0)

    def mix(h, total):
        def one(i):
            mixed = jnp.dot(probs[i], window(vals[h], i), preferred_element_type=jnp.float32)
            live = valid_ref[0, z * ROW + i]
            mixed = jnp.where(slots < live, mixed, 0.0).astype(jnp.bfloat16)
            if h < SHARE - 1:
                return mixed, 0.0
            return mixed, squares(nb[rows_at(i), :], mixed, live) * weights[i]

        def pair(d, e, total):
            first, second = lax.rem(me + d, ROW), lax.rem(me + e, ROW)
            (one_first, err_first), (one_second, err_second) = one(first), one(second)
            outs[h][rows_at(first), :] = one_first
            outs[h][rows_at(second), :] = one_second
            return total + err_first + err_second

        def body(n, total):
            total = pair(2 * n + 2, 2 * n + 3, total)

            @pl.when(n > 0)
            def _():
                back_copy(h, 2 * n, me).start()
                back_copy(h, 2 * n + 1, me).start()
            if h + 1 < SHARE:
                forward_one(SHARE + h + 1, 2 * n + 1)
                forward_one(SHARE + h + 1, 2 * n + 2)
            return total
        total = lax.fori_loop(0, ROW // 2 - 1, body, total)
        total = pair(1, 0, total)
        for d in (ROW - 2, ROW - 1, 1):
            back_copy(h, d, me).start()
        return total

    def error(h):
        def body(d, total):
            r = sender(d)
            return total + squares(nxt[:, columns(r, h)], got[:, columns(r, h)], own_valid)
        return lax.fori_loop(0, ROW, body, jnp.zeros(TILE, jnp.float32)) * weights[me]

    def whole_back(h):
        part = outs[h].at[pl.ds(0, (ROW - 1) * BLK), :]
        return pltpu.make_async_remote_copy(
            src_ref=part, dst_ref=part, send_sem=os_.at[h], recv_sem=or_.at[h],
            device_id=row_dev(lax.rem(me + 1, ROW)), device_id_type=MESH)

    def wait_back(h):
        home_copy(h).wait()
        whole_back(h).wait_recv()

    forward(0)
    pl.semaphore_wait(word.at[0], len(across))
    tell(1, across[:2])
    forward(SHARE)
    for n in range(1, hops - 1):
        pl.semaphore_wait(word.at[n], 2)
        tell(n + 1, across[:2] if n < hops - 2 else [g_dev(d) for d in range(1, ng)])
    acc = jnp.zeros(TILE, jnp.float32)
    for h in range(SHARE):
        wait_share(2 * SHARE + h)
        if h == 1:
            lax.fori_loop(0, ROW, weigh, 0)
        if h == SHARE - 1:
            wait_share(LAST)
        wait_halo(h)
        score(h)
        if h == SHARE - 1:
            latent.wait()
            wait_back(0)
            acc = acc + error(0)
        wait_halo(SHARE + h)
        acc = mix(h, acc)
        home_copy(h).start()
    wait_back(1)
    acc = acc + error(1)
    pl.semaphore_wait(word.at[hops - 1], ng - 1)

    def exchange(buf, stage, place, count, device, between):
        def start(p, carry):
            far = 1 + lax.rem(p + count // 2 - 2, count - 1)
            pltpu.make_async_remote_copy(
                src_ref=buf.at[place], dst_ref=buf.at[place], send_sem=rs.at[stage], recv_sem=rr.at[stage],
                device_id=device(far), device_id_type=MESH).start()
            return carry
        lax.fori_loop(1, count, start, 0)
        between()
        whole = pltpu.make_async_remote_copy(
            src_ref=buf.at[pl.ds(0, count - 1)], dst_ref=buf.at[pl.ds(0, count - 1)],
            send_sem=rs.at[stage], recv_sem=rr.at[stage], device_id=device(1), device_id_type=MESH)
        whole.wait_recv()
        total = jnp.sum(buf[...], axis=0)
        return total, whole.wait_send

    def drain():
        for kind in range(3 * SHARE + 1):
            whole_share(kind).wait_send()
        for kind in range(2 * SHARE):
            whole_halo(kind, True).wait_send()
        for h in range(SHARE):
            whole_back(h).wait_send()

    red_zg[z * ng + g] = jnp.sum(acc, axis=0, keepdims=True)
    home = pltpu.make_async_copy(got, out_hbm.at[0], misc.at[1])

    def rest():
        wait_back(SHARE - 1)
        home.start()
    def plane_dev(p):
        return {"z": lax.rem(z + p // ng, nz), "grp": lax.rem(g + lax.rem(p, ng), ng)}

    acc, sent_plane = exchange(
        red_zg, 0, z * ng + g,
        nz * ng, plane_dev, rest)
    red_x[me] = acc
    acc, sent_row = exchange(
        red_x, 1, me, ROW, lambda p: row_dev(lax.rem(me + p, ROW)),
        drain)
    loss_ref[0, 0] = jnp.sum(acc)
    sent_plane()
    sent_row()
    home.wait()


def solution(mesh):
    ng = mesh.shape["grp"]
    nz = mesh.shape["tok"] // ROW
    finer = Mesh(mesh.devices.reshape(nz, 4, 2, ng), ("z", "x", "c", "grp"))
    tok = ("z", "x", "c")
    big = P("grp", tok, None)
    small = P("grp", None)
    dma = pltpu.SemaphoreType.DMA
    wide = pltpu.VMEM((3 * ROW, BLK, HEAD), jnp.bfloat16)
    row = pltpu.VMEM((ROW * BLK, HEAD), jnp.bfloat16)
    whole = pltpu.VMEM((BLK, D), jnp.bfloat16)
    anywhere = pl.BlockSpec(memory_space=pl.ANY)
    scalars = pl.BlockSpec(memory_space=pltpu.SMEM)


    def on_device(*args):
        out, loss = pl.pallas_call(
            functools.partial(kernel, (nz, ng)),
            out_shape=(jax.ShapeDtypeStruct((1, BLK, D), jnp.bfloat16),
                       jax.ShapeDtypeStruct((1, 1), jnp.float32)),
            in_specs=[anywhere] * 4 + [scalars] * 4,
            out_specs=(anywhere, scalars),
            scratch_shapes=[wide] * 6 + [row] * 7 + [
                pltpu.VMEM((ROW, BLK, SPAN), jnp.bfloat16), whole, whole,
                pltpu.VMEM((ROW, 8, 128), jnp.float32),
                pltpu.SMEM((ROW,), jnp.int32), pltpu.SMEM((ROW * MAXB,), jnp.int32),
                pltpu.VMEM((nz * ng, 1, 128), jnp.float32), pltpu.VMEM((ROW, 1, 128), jnp.float32),
                dma((LAST + 1,)), dma((2 * SHARE, ROW)), dma((SHARE + 1,)), dma((LAST + 1 + SHARE,)),
                dma((2 * SHARE,)), dma((2 * SHARE, 2)), dma((SHARE,)), dma((SHARE,)), dma((2,)),
                dma((2,)), dma((2,)),
                pltpu.SemaphoreType.REGULAR((nz // 2,))],
            compiler_params=pltpu.CompilerParams(
                collective_id=0, has_side_effects=True),
        )(*args)
        return out, loss.reshape(())

    return jax.shard_map(
        on_device, mesh=finer, in_specs=(big,) * 4 + (small,) * 4,
        out_specs=(big, P()), check_vma=False)
```

```python
import functools
import math

import jax
import jax.numpy as jnp
from jax import lax
from jax.experimental import pallas as pl
from jax.experimental.pallas import tpu as pltpu
from jax.sharding import Mesh
from jax.sharding import PartitionSpec as P

D = 3072
HEADS = 24
HEAD = 128
BLK = 128
MAXB = 8
ROW = 8
SHARE = HEADS // ROW
SPAN = MAXB * BLK
MASKED = -1e30
TILE = (8, 128)
LAST = 3 * SHARE
MESH = pl.DeviceIdType.MESH


def rows_at(block):
    return pl.ds(pl.multiple_of(block * BLK, BLK), BLK)


def kernel(sizes, q_hbm, k_hbm, v_hbm, next_hbm, *rest):
    small_hbm, rest = rest[:4], rest[4:]
    (out_hbm, loss_ref, kb0, kb1, kb2, vb0, vb1, vb2, qb0, qb1, qb2, ob0, ob1, ob2, nb,
     probs, got, nxt, weights, first_ref, live_ref, red_zg, red_x,
     xs, xr, qr, own, zs, zr, os_, or_, misc, rs, rr, word,
     clip_ref, valid_ref, group_ref, reward_ref, small) = rest
    rows = [pltpu.make_async_copy(a, b, small.at[n]) for n, (a, b) in enumerate(
        zip(small_hbm, (clip_ref, valid_ref, group_ref, reward_ref)))]
    for copy in rows:
        copy.start()
    nz, ng = sizes
    total_blocks = nz * ROW
    clips = clip_ref.shape[1]
    z, x, c, g = (lax.axis_index(a) for a in ("z", "x", "c", "grp"))
    me = x * 2 + c
    keys, vals, qrys, outs = (kb0, kb1, kb2), (vb0, vb1, vb2), (qb0, qb1, qb2), (ob0, ob1, ob2)

    def row_dev(r):
        return {"x": r // 2, "c": lax.rem(r, 2)}

    def z_dev(dz):
        return {"z": lax.rem(z + dz, nz)}

    def g_dev(dg):
        return {"grp": lax.rem(g + dg, ng)}

    def source(kind):
        return (k_hbm, v_hbm, q_hbm, next_hbm)[kind // SHARE]

    def landing(kind, s):
        h = head_of(kind)
        if kind == LAST:
            return nb.at[rows_at(s), :]
        if kind < 2 * SHARE:
            return (keys, vals)[kind // SHARE][h].at[ROW + s]
        return qrys[h].at[rows_at(s), :]

    def head_of(kind):
        return SHARE - 1 if kind == LAST else kind % SHARE

    def columns(r, h):
        return pl.ds(pl.multiple_of((r * SHARE + h) * HEAD, HEAD), HEAD)

    def share_copy(kind, d, s):
        r = lax.rem(me + d, ROW)
        return pltpu.make_async_remote_copy(
            src_ref=source(kind).at[0, :, columns(r, head_of(kind))],
            dst_ref=landing(kind, s),
            send_sem=xs.at[kind], recv_sem=xr.at[kind, d] if kind < 2 * SHARE else qr.at[kind - 2 * SHARE],
            device_id=row_dev(r), device_id_type=MESH)

    def whole_share(kind):
        part = qb0.at[pl.ds(0, (ROW - 1) * BLK), :]
        return pltpu.make_async_remote_copy(
            src_ref=part, dst_ref=part, send_sem=xs.at[kind], recv_sem=qr.at[max(kind - 2 * SHARE, 0)],
            device_id=row_dev(lax.rem(me + 1, ROW)), device_id_type=MESH)

    def own_copy(kind):
        return pltpu.make_async_copy(
            source(kind).at[0, :, columns(me, head_of(kind))], landing(kind, me), own.at[kind])

    def nth(t):
        return 1 + lax.rem(t + 6 * c, ROW - 1)

    def send_share(kind):
        def body(t, carry):
            share_copy(kind, nth(t), me).start()
            return carry
        lax.fori_loop(1, ROW - 1, body, 0)

    def sender(d):
        return lax.rem(me + ROW - d, ROW)

    def halo_copy(kind, s, d, up, own):
        buf = (keys, vals)[kind // SHARE][kind % SHARE]
        return pltpu.make_async_remote_copy(
            src_ref=source(kind).at[0, :, columns(me, kind % SHARE)] if own else buf.at[ROW + s],
            dst_ref=buf.at[s if up else 2 * ROW + s],
            send_sem=zs.at[kind], recv_sem=zr.at[kind, 0 if up else 1],
            device_id=z_dev(1 if up else nz - 1), device_id_type=MESH)

    def for_halo(kind, s, d, act, own=False):
        @pl.when(s != 0)
        def _():
            act(halo_copy(kind, s, d, True, own))

        @pl.when(s != ROW - 1)
        def _():
            act(halo_copy(kind, s, d, False, own))

    def rnth(t):
        return 1 + lax.rem(t + 6 * (1 - c), ROW - 1)

    def forward_one(kind, t):
        d = rnth(t)
        s = sender(d)
        share_copy(kind, d, s).wait_recv()
        for_halo(kind, s, d, lambda copy: copy.start())

    def forward(kind):
        def body(t, carry):
            forward_one(kind, t)
            return carry
        lax.fori_loop(1, ROW - 1, body, 0)

    def whole_halo(kind, up):
        buf = (keys, vals)[kind // SHARE][kind % SHARE]
        both = buf.at[pl.ds(0, 2 * (ROW - 1))]
        side = buf.at[pl.ds(1 if up else 2 * ROW, ROW - 1)]
        return pltpu.make_async_remote_copy(
            src_ref=both, dst_ref=side, send_sem=zs.at[kind], recv_sem=zr.at[kind, 0 if up else 1],
            device_id=z_dev(1 if up else nz - 1), device_id_type=MESH)

    def wait_halo(kind):
        own_copy(kind).wait()
        whole_halo(kind, True).wait_recv()
        whole_halo(kind, False).wait_recv()

    def wait_share(kind):
        own_copy(kind).wait()
        whole_share(kind).wait_recv()

    barrier = pltpu.get_barrier_semaphore()
    across = [z_dev(1), z_dev(nz - 1), g_dev(1), g_dev(ng - 1)]

    def greet(d, carry):
        pl.semaphore_signal(barrier, inc=1, device_id=row_dev(lax.rem(me + d, ROW)), device_id_type=MESH)
        return carry
    for device in across:
        pl.semaphore_signal(barrier, inc=1, device_id=device, device_id_type=MESH)
    lax.fori_loop(1, ROW, greet, 0)
    pl.semaphore_wait(barrier, ROW - 1 + len(across))

    def tell(n, devices):
        for device in devices:
            pl.semaphore_signal(word.at[n], inc=1, device_id=device, device_id_type=MESH)

    hops = nz // 2
    tell(0, across)

    order = (0, 3, 1, 6, 4, 2, 7, 5, 8, LAST)
    streams = (0, 3, 1, 4, 2, 5)
    send_share(order[0])
    for kind in streams:
        share_copy(kind, nth(0), me).start()
    send_share(order[1])
    for kind in streams:
        for_halo(kind, me, 0, lambda copy: copy.start(), own=True)
    for kind in streams:
        forward_one(kind, 0)
    for kind in order[2:]:
        send_share(kind)
    for kind in order:
        if kind not in streams:
            share_copy(kind, nth(0), me).start()
        own_copy(kind).start()
    latent = pltpu.make_async_copy(next_hbm.at[0], nxt, misc.at[0])
    latent.start()

    def clip_of(block):
        def body(i, carry):
            begin, start, count, own = carry
            size = clip_ref[0, i]
            inside = (block >= begin) & (block < begin + size)
            return (begin + size, jnp.where(inside, begin, start), jnp.where(inside, size, count),
                    jnp.where(inside, i, own))
        zero = jnp.int32(0)
        _, start, count, own = lax.fori_loop(0, clips, body, (zero, zero, zero, zero))
        return start, count, own

    for copy in rows:
        copy.wait()

    def note(i, carry):
        start, count, _ = clip_of(z * ROW + i)
        first_ref[i] = jnp.clip(start - (z * ROW - ROW), 0, 2 * ROW)
        for j in range(MAXB):
            live = valid_ref[0, jnp.minimum(start + j, total_blocks - 1)]
            live_ref[i * MAXB + j] = jnp.where(j < count, live, 0)
        return carry
    lax.fori_loop(0, ROW, note, 0)

    def weigh(b, carry):
        start, count, own = clip_of(z * ROW + b)
        group = group_ref[0, own]

        def member(i, sums):
            total, number = sums
            same = group_ref[0, i] == group
            return (total + jnp.where(same, reward_ref[0, i], 0.0), number + jnp.where(same, 1.0, 0.0))
        total, number = lax.fori_loop(0, clips, member, (jnp.float32(0), jnp.float32(0)))
        tokens = jnp.int32(0)
        for j in range(MAXB):
            tokens = tokens + live_ref[b * MAXB + j]
        mean = jnp.full(TILE, total) / jnp.full(TILE, jnp.maximum(number, 1.0))
        adv = jnp.full(TILE, reward_ref[0, own]) - mean
        weights[b] = adv / jnp.full(TILE, (2.0 * D) * tokens.astype(jnp.float32))
        return carry

    own_valid = valid_ref[0, z * ROW + me]
    lanes = lax.broadcasted_iota(jnp.int32, (1, BLK), 1)
    slots = lax.broadcasted_iota(jnp.int32, (BLK, HEAD), 0)

    def window(buf, i):
        first = first_ref[i]
        return jnp.concatenate([buf[first + j] for j in range(MAXB)], axis=0)

    def score(h, beside):
        def one(i):
            query = qrys[h][rows_at(i), :]
            key = window(keys[h], i)
            scores = lax.dot_general(query, key, (((1,), (1,)), ((), ())),
                                     preferred_element_type=jnp.float32)
            bias = []
            for j in range(MAXB):
                live = live_ref[i * MAXB + j]
                bias.append(jnp.where(lanes < live, 0.0, MASKED))
            scores = scores * (1.0 / math.sqrt(HEAD)) + jnp.concatenate(bias, axis=1)
            top = jnp.max(scores, axis=-1, keepdims=True)
            expo = jnp.exp(scores - top)
            inverse = 1.0 / jnp.sum(expo, axis=-1, keepdims=True)
            return (expo * inverse).astype(jnp.bfloat16)

        def body(n, carry):
            if beside is not None:
                @pl.when(n < ROW // 2 - 1)
                def _():
                    forward_one(beside, 2 * n + 1)
                    forward_one(beside, 2 * n + 2)
            first, second = one(2 * n), one(2 * n + 1)
            probs[2 * n] = first
            probs[2 * n + 1] = second
            return carry
        lax.fori_loop(0, ROW // 2, body, 0)

    def back_copy(h, d, r):
        return pltpu.make_async_remote_copy(
            src_ref=outs[h].at[rows_at(lax.rem(me + d, ROW)), :],
            dst_ref=got.at[:, columns(r, h)],
            send_sem=os_.at[h], recv_sem=or_.at[h],
            device_id=row_dev(lax.rem(me + d, ROW)), device_id_type=MESH)

    def home_copy(h):
        return pltpu.make_async_copy(
            outs[h].at[rows_at(me), :], got.at[:, columns(me, h)], own.at[LAST + 1 + h])

    def squares(latent_block, velocity_block, live):
        diff = latent_block.astype(jnp.float32) - velocity_block.astype(jnp.float32)
        diff = jnp.where(slots < live, diff, 0.0)
        return jnp.sum((diff * diff).reshape(BLK // 8, 8, HEAD), axis=0)

    def mix(h, total, beside):
        def one(i):
            mixed = jnp.dot(probs[i], window(vals[h], i), preferred_element_type=jnp.float32)
            live = valid_ref[0, z * ROW + i]
            mixed = jnp.where(slots < live, mixed, 0.0).astype(jnp.bfloat16)
            if h < SHARE - 1:
                return mixed, 0.0
            return mixed, squares(nb[rows_at(i), :], mixed, live) * weights[i]

        def pair(d, e, total):
            first, second = lax.rem(me + d, ROW), lax.rem(me + e, ROW)
            (one_first, err_first), (one_second, err_second) = one(first), one(second)
            outs[h][rows_at(first), :] = one_first
            outs[h][rows_at(second), :] = one_second
            return total + err_first + err_second

        def body(n, total):
            total = pair(2 * n + 2, 2 * n + 3, total)

            @pl.when(n > 0)
            def _():
                back_copy(h, 2 * n, me).start()
                back_copy(h, 2 * n + 1, me).start()
            if beside is not None:
                forward_one(beside, 2 * n + 1)
                forward_one(beside, 2 * n + 2)
            return total
        total = lax.fori_loop(0, ROW // 2 - 1, body, total)
        total = pair(1, 0, total)
        for d in (ROW - 2, ROW - 1, 1):
            back_copy(h, d, me).start()
        return total

    def error(h):
        def body(d, total):
            r = sender(d)
            return total + squares(nxt[:, columns(r, h)], got[:, columns(r, h)], own_valid)
        return lax.fori_loop(0, ROW, body, jnp.zeros(TILE, jnp.float32)) * weights[me]

    def whole_back(h):
        part = outs[h].at[pl.ds(0, (ROW - 1) * BLK), :]
        return pltpu.make_async_remote_copy(
            src_ref=part, dst_ref=part, send_sem=os_.at[h], recv_sem=or_.at[h],
            device_id=row_dev(lax.rem(me + 1, ROW)), device_id_type=MESH)

    def wait_back(h):
        home_copy(h).wait()
        whole_back(h).wait_recv()

    forward(0)
    pl.semaphore_wait(word.at[0], len(across))
    tell(1, across[:2])
    forward(SHARE)
    for n in range(1, hops - 1):
        pl.semaphore_wait(word.at[n], 2)
        tell(n + 1, across[:2] if n < hops - 2 else [g_dev(d) for d in range(1, ng)])
    acc = jnp.zeros(TILE, jnp.float32)
    for h in range(SHARE):
        if h == SHARE - 1:
            lax.fori_loop(0, ROW, weigh, 0)
        wait_share(2 * SHARE + h)
        wait_halo(h)
        score(h, (1, 5, None)[h])
        if h == SHARE - 1:
            latent.wait()
            wait_back(0)
            acc = acc + error(0)
            wait_share(LAST)
        wait_halo(SHARE + h)
        acc = mix(h, acc, (4, None, None)[h])
        home_copy(h).start()
        if h == 0:
            forward(2)
    wait_back(1)
    acc = acc + error(1)
    pl.semaphore_wait(word.at[hops - 1], ng - 1)

    def exchange(buf, stage, place, count, device, between):
        def start(p, carry):
            far = 1 + lax.rem(p + count // 2 - 2, count - 1)
            pltpu.make_async_remote_copy(
                src_ref=buf.at[place], dst_ref=buf.at[place], send_sem=rs.at[stage], recv_sem=rr.at[stage],
                device_id=device(far), device_id_type=MESH).start()
            return carry
        lax.fori_loop(1, count, start, 0)
        between()
        whole = pltpu.make_async_remote_copy(
            src_ref=buf.at[pl.ds(0, count - 1)], dst_ref=buf.at[pl.ds(0, count - 1)],
            send_sem=rs.at[stage], recv_sem=rr.at[stage], device_id=device(1), device_id_type=MESH)
        whole.wait_recv()
        total = jnp.sum(buf[...], axis=0)
        return total, whole.wait_send

    def drain():
        for kind in range(3 * SHARE + 1):
            whole_share(kind).wait_send()
        for kind in range(2 * SHARE):
            whole_halo(kind, True).wait_send()
        for h in range(SHARE):
            whole_back(h).wait_send()

    red_zg[z * ng + g] = jnp.sum(acc, axis=0, keepdims=True)
    home = pltpu.make_async_copy(got, out_hbm.at[0], misc.at[1])

    def rest():
        wait_back(SHARE - 1)
        home.start()
    def plane_dev(p):
        return {"z": lax.rem(z + p // ng, nz), "grp": lax.rem(g + lax.rem(p, ng), ng)}

    acc, sent_plane = exchange(
        red_zg, 0, z * ng + g,
        nz * ng, plane_dev, rest)
    red_x[me] = acc
    acc, sent_row = exchange(
        red_x, 1, me, ROW, lambda p: row_dev(lax.rem(me + p, ROW)),
        drain)
    loss_ref[0, 0] = jnp.sum(acc)
    sent_plane()
    sent_row()
    home.wait()


def solution(mesh):
    ng = mesh.shape["grp"]
    nz = mesh.shape["tok"] // ROW
    finer = Mesh(mesh.devices.reshape(nz, 4, 2, ng), ("z", "x", "c", "grp"))
    tok = ("z", "x", "c")
    big = P("grp", tok, None)
    small = P("grp", None)
    dma = pltpu.SemaphoreType.DMA
    wide = pltpu.VMEM((3 * ROW, BLK, HEAD), jnp.bfloat16)
    row = pltpu.VMEM((ROW * BLK, HEAD), jnp.bfloat16)
    whole = pltpu.VMEM((BLK, D), jnp.bfloat16)
    anywhere = pl.BlockSpec(memory_space=pl.ANY)
    scalars = pl.BlockSpec(memory_space=pltpu.SMEM)


    def on_device(*args):
        out, loss = pl.pallas_call(
            functools.partial(kernel, (nz, ng)),
            out_shape=(jax.ShapeDtypeStruct((1, BLK, D), jnp.bfloat16),
                       jax.ShapeDtypeStruct((1, 1), jnp.float32)),
            in_specs=[anywhere] * 8,
            out_specs=(anywhere, scalars),
            scratch_shapes=[wide] * 6 + [row] * 7 + [
                pltpu.VMEM((ROW, BLK, SPAN), jnp.bfloat16), whole, whole,
                pltpu.VMEM((ROW, 8, 128), jnp.float32),
                pltpu.SMEM((ROW,), jnp.int32), pltpu.SMEM((ROW * MAXB,), jnp.int32),
                pltpu.VMEM((nz * ng, 1, 128), jnp.float32), pltpu.VMEM((ROW, 1, 128), jnp.float32),
                dma((LAST + 1,)), dma((2 * SHARE, ROW)), dma((SHARE + 1,)), dma((LAST + 1 + SHARE,)),
                dma((2 * SHARE,)), dma((2 * SHARE, 2)), dma((SHARE,)), dma((SHARE,)), dma((2,)),
                dma((2,)), dma((2,)),
                pltpu.SemaphoreType.REGULAR((nz // 2,)),
                *(pltpu.SMEM(a.shape, a.dtype) for a in args[4:]), dma((4,))],
            compiler_params=pltpu.CompilerParams(
                collective_id=0, has_side_effects=True),
        )(*args)
        return out, loss.reshape(())

    return jax.shard_map(
        on_device, mesh=finer, in_specs=(big,) * 4 + (small,) * 4,
        out_specs=(big, P()), check_vma=False)
```
